128 devices in a mesh: row: 8 (over z, x_hi), col: 16 (over x_lo, y, core).
Axes of the slice: x: 4 (x_hi: 2, x_lo: 2; x = x_hi * 2 + x_lo), y: 4, z: 4, core: 2. Of those that a mesh axis runs over, the one named last changes fastest.
Arguments:
- embeddings: bfloat16 [32768, 768], P(('row', 'col'))
- spread: bfloat16 [32768], P(('row', 'col')), may hold values from 1 to 16
- features: bfloat16 [32768, 256], P(('row', 'col')), may hold values from -160 to 160
- block_list: int32 [256], replicated, may hold values from 0 to 63
- list_pairs: int32 [64, 64], replicated, may hold values from 0 to 1, as said below
Outputs:
- smoothed: float32 [32768, 256], P(('row', 'col'))
The draws below stay inside these ranges and needn't reach their ends.
Inputs may be any that keep to these rules, and one draw needn't show every extreme that they name: `list_pairs`: symmetric, with ones on the diagonal.
All inputs are finite; a program needn't handle non-finite values.
Results may differ from the reference program's by a relative error of at most 0.0029.
Values may be sent and summed in bfloat16 or wider, within the bound.
A program may use at most 64 MiB of HBM per device.

```python
import math
import jax
import jax.numpy as jnp
import numpy as np
from jax import lax

E = 768
F = 256
BLK = 128
LISTS = 64
N = 32768
NB = 256


def draw_embeddings(key, part):
    key_base = jax.random.fold_in(key, 11)
    key_values = jax.random.fold_in(key_base, 0)
    values = jnp.clip(jax.random.normal(key_values, (N, E), jnp.float32), -4.0, 4.0)
    return (values / jnp.sqrt(jnp.float32(E))).astype(jnp.bfloat16)


def draw_list_pairs(key, part):
    key_base = jax.random.fold_in(key, 23)
    picks = (jax.random.randint(key_base, (LISTS, LISTS), 0, 4) == 0).astype(jnp.int32)
    upper = jnp.triu(picks, 1)
    table = upper + upper.T + jnp.eye(LISTS, dtype=jnp.int32)
    return table.astype(jnp.int32)


def plant(entries, stream_key, low, largest):
    longest = entries.shape.index(max(entries.shape))
    spots = []
    for shift in (0, 1):
        where = [jax.random.randint(jax.random.fold_in(stream_key, axis), (), 0, length) for axis, length in enumerate(entries.shape)]
        where[longest] = (where[longest] + shift) % entries.shape[longest]
        spots.append(tuple(where))
    return entries.at[spots[0]].set(low).at[spots[1]].set(largest)


def block_scale(key, shape, cuts, smallest, largest):
    def one(axis_at, blocks):
        heights = jax.random.uniform(jax.random.fold_in(jax.random.fold_in(key, 6), axis_at), (blocks,), jnp.float32, smallest / len(cuts), largest / len(cuts))
        return jnp.repeat(jnp.exp(heights), shape[axis_at] // blocks).reshape((-1,) + (1,) * (len(shape) - axis_at - 1))

    level = one(*cuts[0])
    for cut in cuts[1:]:
        level = level * one(*cut)
    return level


def rank_bounds(amount, lean):
    weights = [(1 << 20) // math.isqrt(grade ** lean) + 1 for grade in range(1, amount + 1)]
    width = 1 + sum(weights) // (1 << 30)
    return np.cumsum(np.array([max(1, weight // width) for weight in weights]))


def skewed_ids(stream_key, shape, amount, skew):
    grid = rank_bounds(amount, skew)
    pick = jax.random.randint(jax.random.fold_in(stream_key, 1), shape, 0, int(grid[amount - 1]))
    standing = jnp.searchsorted(jnp.asarray(grid, jnp.int32), pick, side="right")
    return jax.random.permutation(jax.random.fold_in(stream_key, 2), amount)[standing].astype(jnp.int32)


def normal_values(own_key, dims, scale, most, pieces=(), held_as=jnp.bfloat16):
    result = jax.random.normal(own_key, dims, jnp.float32) * scale
    if len(pieces) > 0:
        result = block_scale(own_key, dims, pieces, -0.22, 0.18) * result
    return jnp.clip(result, min=-most, max=most).astype(held_as)


def setup_inputs(seed: int = 0) -> dict:
    keys = jax.random.split(jax.random.key(seed), 6)
    embeddings = draw_embeddings(jax.random.fold_in(keys[5], 71), 0)
    spread = jnp.clip(jnp.exp(math.log(16.0) - 2.7725887 * jax.random.uniform(keys[1], (N,), jnp.float32) ** block_scale(keys[1], (N,), ((0, 128),), -0.2, 0.2)), 1.0, 16.0).astype(jnp.bfloat16)
    features = normal_values(keys[2], (N, F), 32.0, 160.0, ((0, 128),))
    block_list = plant(skewed_ids(keys[3], (NB,), LISTS, 2), jax.random.fold_in(keys[3], 3), 0, LISTS - 1).astype(jnp.int32)
    list_pairs = draw_list_pairs(jax.random.fold_in(keys[5], 71), 0)
    return dict(embeddings=embeddings, spread=spread, features=features, block_list=block_list, list_pairs=list_pairs)


def active_table(block_list, list_pairs, row_blocks, col_blocks):
    count = block_list.shape[0]
    lists_onehot = (block_list[:, None] == jnp.arange(LISTS, dtype=jnp.int32)[None, :]).astype(jnp.float32)
    pair_table = list_pairs.astype(jnp.float32)
    row_select = (row_blocks[:, None] == jnp.arange(count, dtype=jnp.int32)[None, :]).astype(jnp.float32)
    col_select = (col_blocks[:, None] == jnp.arange(count, dtype=jnp.int32)[None, :]).astype(jnp.float32)
    row_onehot = jnp.dot(row_select, lists_onehot, precision=lax.Precision.HIGHEST)
    col_onehot = jnp.dot(col_select, lists_onehot, precision=lax.Precision.HIGHEST)
    joined = jnp.dot(row_onehot, pair_table, precision=lax.Precision.HIGHEST)
    return jnp.dot(joined, col_onehot.T, precision=lax.Precision.HIGHEST)


def keep_mask(active, row_ids, col_ids):
    size_rows = row_ids.shape[0]
    col_blocks = active.shape[1]
    expanded = jnp.broadcast_to(active[:, None, :, None], (size_rows // BLK, BLK, col_blocks, BLK))
    expanded = expanded.reshape(size_rows, col_blocks * BLK)
    return expanded * (row_ids[:, None] != col_ids[None, :]).astype(jnp.float32)


def reference(embeddings, spread, features, block_list, list_pairs):
    total = embeddings.shape[0]
    block_rows = math.gcd(total, 512)
    norms = jnp.sum(jnp.square(embeddings.astype(jnp.float32)), axis=1)
    beta = spread.astype(jnp.float32)
    all_ids = jnp.arange(total, dtype=jnp.int32)

    def block_terms(start):
        row_emb = lax.dynamic_slice_in_dim(embeddings, start, block_rows, 0)
        row_norm = lax.dynamic_slice_in_dim(norms, start, block_rows, 0)
        row_beta = lax.dynamic_slice_in_dim(beta, start, block_rows, 0)
        inner = lax.dot_general(row_emb, embeddings, (((1,), (1,)), ((), ())), preferred_element_type=jnp.float32)
        dist = row_norm[:, None] + norms[None, :] - 2.0 * inner
        row_ids = start + jnp.arange(block_rows, dtype=jnp.int32)
        active = active_table(block_list, list_pairs, row_ids[::BLK] // BLK, all_ids[::BLK] // BLK)
        mask = keep_mask(active, row_ids, all_ids)
        near = mask * jnp.exp(-row_beta[:, None] * dist)
        far = mask * jnp.exp(-beta[None, :] * dist)
        return near, far, start

    starts = jnp.arange(total // block_rows, dtype=jnp.int32) * block_rows
    row_totals = lax.map(lambda start: jnp.sum(block_terms(start)[0], axis=1), starts).reshape(total)

    def weighted(start):
        near, far, begin = block_terms(start)
        row_total = lax.dynamic_slice_in_dim(row_totals, begin, block_rows, 0)
        weight = ((near / row_total[:, None] + far / row_totals[None, :]) * 0.5).astype(jnp.bfloat16)
        return jnp.dot(weight, features, preferred_element_type=jnp.float32)

    return lax.map(weighted, starts).reshape(total, features.shape[1])
```

```python
import math

import jax
import jax.numpy as jnp
from jax import lax
from jax.experimental import pallas as pl
from jax.experimental.pallas import tpu as pltpu
from jax.sharding import PartitionSpec as P

BLK = 128
F32 = jnp.float32
BF16 = jnp.bfloat16
LOG2E = math.log2(math.e)
INF = float("inf")
MESH = pl.DeviceIdType.MESH

RECTS = (
    (0, 1, 0, 1),
    (1, 2, 0, 1),
    (0, 3, 1, 2),
    (3, 2, 0, 3),
    (0, 5, 3, 1),
    (0, 5, 4, 1),
    (5, 2, 0, 5),
    (7, 1, 0, 5),
    (0, 8, 5, 2),
    (0, 8, 7, 1),
)


def slot_of(pos):
    low = pos % 4
    return pos + (low == 2).astype(jnp.int32) - (low == 3).astype(jnp.int32)


def kernel(
    x_ref, xt_ref, f_ref, aux_ref, bl_ref, lp_ref, out_ref,
    rx, ct, fb, t_ref, rn, rc, ra, ca, cs, tr, al, ral, cal, cv, w_ref, sr, ob, obr, rl, cl,
    loc, rx_s, rx_r, dd_s, dd_r, ct_s, ct_r, fb_s, fb_r, ax_s, rax_r, cax_r, tr_s, tr_r,
    al_s, ral_r, cal_r, sr_s, sr_r, ob_s, ob_r,
):
    own = x_ref.shape[0]
    wide = x_ref.shape[1]
    half = own // 2
    row = lax.axis_index("row")
    col = lax.axis_index("col")
    xl, y, core = col // 8, (col // 2) % 4, col % 2
    z, xh = row // 2, row % 2

    def rpeer(dx, dy, dk):
        return {"col": ((xl + dx) % 2) * 8 + ((y + dy + 4) % 4) * 2 + (core + dk) % 2}

    def cpeer(dx, dz):
        return {"row": ((z + dz + 4) % 4) * 2 + (xh + dx) % 2}

    locals_ = [
        pltpu.make_async_copy(x_ref, rx.at[0, 0], loc.at[0]),
        pltpu.make_async_copy(xt_ref, ct.at[0], loc.at[1]),
        pltpu.make_async_copy(f_ref, fb.at[0], loc.at[2]),
        pltpu.make_async_copy(aux_ref, ra.at[0, 0], loc.at[3]),
        pltpu.make_async_copy(aux_ref, ca.at[0], loc.at[4]),
    ]
    for c in locals_:
        c.start()

    barrier = pltpu.get_barrier_semaphore()
    for i in range(8):
        for h in range(2):
            if i + h > 0:
                pl.semaphore_signal(
                    barrier, inc=1, device_id=rpeer(i // 4, i % 4, h), device_id_type=MESH
                )
        if i > 0:
            pl.semaphore_signal(barrier, inc=1, device_id=cpeer(i // 4, i % 4), device_id_type=MESH)

    for i in range(8):
        dx, e = i // 4, i % 4
        for h in range(2):
            owner = row * 16 + rpeer(dx, -e, h)["col"]
            for b in range(2):
                rl[i * 4 + h * 2 + b] = bl_ref[owner * 2 + b]
        owner = cpeer(dx, -e)["row"] * 16 + col
        for b in range(2):
            cl[i * 2 + b] = bl_ref[owner * 2 + b]
    cs[...] = jnp.zeros_like(cs)

    for c in locals_:
        c.wait()
    pl.semaphore_wait(barrier, 22)

    started = []

    def remote(src, dst, ssem, rsem, to):
        return pltpu.make_async_remote_copy(
            src_ref=src, dst_ref=dst, send_sem=ssem, recv_sem=rsem, device_id=to, device_id_type=MESH
        )

    def send(make):
        remote(*make()).start()
        started.append(make)

    def arrived(dst, rsem):
        pltpu.make_async_remote_copy(
            src_ref=dst, dst_ref=dst, send_sem=rsem, recv_sem=rsem,
            device_id=rpeer(0, 0, 1), device_id_type=MESH,
        ).wait_recv()

    class Gather:
        def __init__(self, view, ssem, rsem, peer, size):
            self.view, self.ssem, self.rsem, self.peer, self.size = view, ssem, rsem, peer, size

        def parts(self, slot):
            return (
                self.view(slot, 0, self.size // 2),
                self.view(slot, self.size // 2, self.size // 2),
            )

        def whole(self, slot):
            return self.view(slot, 0, self.size)

        def own_x(self):
            send(lambda: (self.whole(0), self.whole(4), self.ssem.at[0], self.rsem.at[4, 0], self.peer(1, 0)))

        def ring(self, base, m):
            send(lambda: (self.whole(base), self.whole(base + 1), self.ssem.at[m], self.rsem.at[base + 1, 0], self.peer(0, 1)))
            send(lambda: (self.whole(base), self.whole(base + 3), self.ssem.at[m + 1], self.rsem.at[base + 3, 0], self.peer(0, -1)))

        def recv(self, slot):
            if slot % 4 == 2:
                a, b = self.parts(slot)
                arrived(a, self.rsem.at[slot, 0])
                arrived(b, self.rsem.at[slot, 1])
            else:
                arrived(self.whole(slot), self.rsem.at[slot, 0])

        def halves(self, base, m):
            send(lambda: (self.parts(base + 1)[0], self.parts(base + 2)[0], self.ssem.at[m], self.rsem.at[base + 2, 0], self.peer(0, 1)))
            send(lambda: (self.parts(base + 3)[1], self.parts(base + 2)[1], self.ssem.at[m + 1], self.rsem.at[base + 2, 1], self.peer(0, -1)))

    rows = Gather(lambda s, lo, n: rx.at[s, 0, pl.ds(lo, n)], rx_s, rx_r, lambda dx, d: rpeer(dx, d, 0), own)
    cols = Gather(lambda s, lo, n: ct.at[s, pl.ds(lo, n)], ct_s, ct_r, cpeer, wide)
    feat = Gather(lambda s, lo, n: fb.at[s, pl.ds(lo, n)], fb_s, fb_r, cpeer, own)

    def sibling(slot):
        send(lambda: (rx.at[slot, 0], rx.at[slot, 1], dd_s.at[slot], dd_r.at[slot], rpeer(0, 0, 1)))

    def spread_out(src, rdst, cdst, ssem, rrecv, crecv):
        for i in range(8):
            dx, e = i // 4, i % 4
            for h in range(2):
                if i + h > 0:
                    send(lambda i=i, h=h, dx=dx, e=e: (src, rdst.at[i, h], ssem.at[i, h], rrecv.at[i, h], rpeer(dx, e, h)))
            if i > 0:
                send(lambda i=i, dx=dx, e=e: (src, cdst.at[i], ssem.at[i, 2], crecv.at[i], cpeer(dx, e)))

    def lanes(a8, k):
        return jnp.broadcast_to(jnp.transpose(a8)[:, k : k + 1], (own, 128))

    def row_terms(i, h):
        a8 = ra[i, h]
        rn[i, h * own : (h + 1) * own, :] = lanes(a8, 0)
        rc[i, h * own : (h + 1) * own, :] = lanes(a8, 1)

    def row_ready(i):
        for h in range(2):
            if i + h > 0:
                arrived(ra.at[i, h], rax_r.at[i, h])
            row_terms(i, h)
        arrived(rx.at[i, 1], dd_r.at[i])

    def col_ready(i):
        if i > 0:
            arrived(ca.at[i], cax_r.at[i])

    def pair(i, q, diagonal):
        lhs = rx[i].reshape(2 * own, wide)
        s = jnp.dot(lhs, ct[q], preferred_element_type=F32)
        acc0 = jnp.zeros((8, BLK), F32)
        acc = [acc0, acc0]
        for b in range(2 * own // BLK):
            base = []
            for cb in range(own // BLK):
                on = lp_ref[rl[i * 4 + b], cl[q * 2 + cb]]
                pen = jnp.where(on > 0, 0.0, INF).astype(F32)
                base.append(ca[q, 0:1, cb * BLK : (cb + 1) * BLK] + pen)
            for r8 in range(BLK // 8):
                lo = b * BLK + r8 * 8
                r_n = rn[i, lo : lo + 8, :]
                for cb in range(own // BLK):
                    d = (r_n + base[cb]) - s[lo : lo + 8, cb * BLK : (cb + 1) * BLK]
                    if diagonal and b == cb:
                        at_r = r8 * 8 + lax.broadcasted_iota(jnp.int32, (8, BLK), 0)
                        at_c = lax.broadcasted_iota(jnp.int32, (8, BLK), 1)
                        d = jnp.where(at_r == at_c, INF, d)
                    t_ref[i, lo : lo + 8, pl.ds(pl.multiple_of(q * own + cb * BLK, BLK), BLK)] = d
                    acc[cb] = acc[cb] + jnp.exp2(d * ca[q, 1:2, cb * BLK : (cb + 1) * BLK])
        cs[q] = cs[q] + jnp.concatenate(acc, axis=1)

    rows.ring(0, 1)
    cols.ring(0, 1)
    cols.own_x()
    rows.own_x()
    sibling(0)
    spread_out(aux_ref, ra, ca, ax_s, rax_r, cax_r)

    row_ready(0)
    pair(0, 0, True)

    def before(k):
        if k == 1:
            for s in (1, 3):
                rows.recv(s)
            rows.halves(0, 3)
            rows.recv(4)
            rows.ring(4, 5)
            for s in (1, 3):
                cols.recv(s)
            cols.halves(0, 3)
            for s in (1, 3, 4):
                sibling(s)
            for s in (1, 3):
                row_ready(s)
                col_ready(s)
        if k == 3:
            rows.recv(2)
            sibling(2)
            row_ready(4)
            row_ready(2)
        if k == 4:
            cols.recv(2)
            col_ready(2)
            feat.ring(0, 1)
        if k == 5:
            cols.recv(4)
            cols.ring(4, 5)
            col_ready(4)
            feat.own_x()
        if k == 6:
            for s in (5, 7):
                rows.recv(s)
            rows.halves(4, 7)
            for s in (5, 7):
                sibling(s)
            for s in (5, 7):
                row_ready(s)
        if k == 7:
            rows.recv(6)
            sibling(6)
            row_ready(6)
        if k == 8:
            for s in (5, 7):
                cols.recv(s)
            cols.halves(4, 7)
            for s in (1, 3):
                feat.recv(s)
            feat.halves(0, 3)
            feat.recv(4)
            feat.ring(4, 5)
            for s in (5, 7):
                col_ready(s)
        if k == 9:
            cols.recv(6)
            col_ready(6)

    def rect(k, carry):
        here = [(k == j).astype(jnp.int32) for j in range(1, len(RECTS))]
        first, count_r, lead, count_c = (
            sum(m * r[f] for m, r in zip(here, RECTS[1:])) for f in range(4)
        )
        for j in range(1, len(RECTS)):
            @pl.when(k == j)
            def _():
                before(j)

        def inner_c(cc, carry2):
            q = slot_of(lead + cc)

            def inner_r(rr, carry3):
                pair(slot_of(first + rr), q, False)
                return carry3

            return lax.fori_loop(0, count_r, inner_r, carry2)

        return lax.fori_loop(0, count_c, inner_c, carry)

    lax.fori_loop(1, len(RECTS), rect, 0)

    for q in range(1, 8):
        send(lambda q=q: (cs.at[q], tr.at[(q // 4) * 4 + (4 - q % 4) % 4], tr_s.at[q], tr_r.at[(q // 4) * 4 + (4 - q % 4) % 4], cpeer(q // 4, -(q % 4))))
    for s in (5, 7):
        feat.recv(s)
    feat.halves(4, 7)
    total = cs[0]
    for q in range(1, 8):
        arrived(tr.at[q], tr_r.at[q])
        total = total + tr[q]
    al[...] = jnp.broadcast_to(0.5 / jnp.sum(total, axis=0, keepdims=True), al.shape)
    ral[0, 0] = al[...]
    cal[0] = al[...]
    spread_out(al, ral, cal, al_s, ral_r, cal_r)
    for q in range(8):
        if q > 0:
            arrived(cal.at[q], cal_r.at[q])
        cv[0:1, q * own : (q + 1) * own] = ca[q, 1:2, :]
        cv[1:2, q * own : (q + 1) * own] = cal[q, 0:1, :]
    for i in range(8):
        for h in range(2):
            if i + h > 0:
                arrived(ral.at[i, h], ral_r.at[i, h])
    for s in (2, 6):
        feat.recv(s)

    total_cols = 8 * own
    step_r, step_c = 64, 256

    def weigh(i, h):
        ar = jnp.transpose(ral[i, h])[:, 0:1]
        for r in range(own // step_r):
            a_r = jnp.broadcast_to(ar[r * step_r : (r + 1) * step_r], (step_r, 128))
            a_r = jnp.concatenate([a_r] * (step_c // 128), axis=1)
            c_r = rc[i, h * own + r * step_r : h * own + (r + 1) * step_r, :]
            c_r = jnp.concatenate([c_r] * (step_c // 128), axis=1)
            for c in range(total_cols // step_c):
                sl = slice(c * step_c, (c + 1) * step_c)
                d = t_ref[i, h * own + r * step_r : h * own + (r + 1) * step_r, sl]
                v = jnp.exp2(d * c_r) * a_r + jnp.exp2(d * cv[0:1, sl]) * cv[1:2, sl]
                w_ref[h, r * step_r : (r + 1) * step_r, sl] = v.astype(BF16)

    def back(slot):
        return slot - slot % 4 + (4 - slot % 4) % 4

    def out_step(j, carry):
        i = slot_of(7 - j)
        dx, e = i // 4, i % 4
        feats = fb[...].reshape(total_cols, fb.shape[2])
        weigh(i, 1)
        other = jnp.dot(w_ref[1], feats, preferred_element_type=F32)
        t_ref[i, own : 2 * own, 0 : fb.shape[2]] = other
        pltpu.make_async_remote_copy(
            src_ref=t_ref.at[i, pl.ds(own, own), pl.ds(0, fb.shape[2])], dst_ref=sr.at[i],
            send_sem=sr_s.at[i], recv_sem=sr_r.at[i], device_id=rpeer(0, 0, 1), device_id_type=MESH,
        ).start()
        weigh(i, 0)
        mine = jnp.dot(w_ref[0], feats, preferred_element_type=F32)
        arrived(sr.at[i], sr_r.at[i])
        sr[i] = sr[i] + mine

        @pl.when(j < 7)
        def _():
            ob[i] = sr[i].astype(BF16)
            pltpu.make_async_remote_copy(
                src_ref=ob.at[i], dst_ref=obr.at[back(i)], send_sem=ob_s.at[i], recv_sem=ob_r.at[back(i)],
                device_id=rpeer(dx, 4 - e, 0), device_id_type=MESH,
            ).start()
        return carry

    lax.fori_loop(0, 8, out_step, 0)
    result = sr[0]
    for i in range(1, 8):
        arrived(obr.at[i], ob_r.at[i])
        result = result + obr[i].astype(F32)
    out_ref[...] = result
    for make in started:
        remote(*make()).wait_send()
    for i in range(8):
        pltpu.make_async_remote_copy(
            src_ref=t_ref.at[i, pl.ds(own, own), pl.ds(0, fb.shape[2])], dst_ref=sr.at[i],
            send_sem=sr_s.at[i], recv_sem=sr_r.at[i], device_id=rpeer(0, 0, 1), device_id_type=MESH,
        ).wait_send()
        if i > 0:
            pltpu.make_async_remote_copy(
                src_ref=ob.at[i], dst_ref=obr.at[i], send_sem=ob_s.at[i], recv_sem=ob_r.at[i],
                device_id=rpeer(0, 0, 1), device_id_type=MESH,
            ).wait_send()


def shards(embeddings, spread, features, block_list, list_pairs):
    own, wide = embeddings.shape
    feats = features.shape[1]
    norm = jnp.sum(jnp.square(embeddings.astype(F32)), axis=1)
    rate = spread.astype(F32) * (-LOG2E)
    aux = jnp.concatenate([norm[None], rate[None], jnp.zeros((6, own), F32)], axis=0)
    twice = (embeddings * jnp.asarray(2.0, BF16)).T
    anywhere = pl.BlockSpec(memory_space=pl.ANY)
    scalars = pl.BlockSpec(memory_space=pltpu.SMEM)
    vmem, dma = pltpu.VMEM, pltpu.SemaphoreType.DMA
    return pl.pallas_call(
        kernel,
        out_shape=jax.ShapeDtypeStruct((own, feats), F32),
        in_specs=[anywhere] * 4 + [scalars] * 2,
        out_specs=pl.BlockSpec(memory_space=pltpu.VMEM),
        scratch_shapes=[
            vmem((8, 2, own, wide), BF16),
            vmem((8, wide, own), BF16),
            vmem((8, own, feats), BF16),
            vmem((8, 2 * own, 8 * own), F32),
            vmem((8, 2 * own, 128), F32),
            vmem((8, 2 * own, 128), F32),
            vmem((8, 2, 8, own), F32),
            vmem((8, 8, own), F32),
            vmem((8, 8, own), F32),
            vmem((8, 8, own), F32),
            vmem((8, own), F32),
            vmem((8, 2, 8, own), F32),
            vmem((8, 8, own), F32),
            vmem((8, 8 * own), F32),
            vmem((2, own, 8 * own), BF16),
            vmem((8, own, feats), F32),
            vmem((8, own, feats), BF16),
            vmem((8, own, feats), BF16),
            pltpu.SMEM((32,), jnp.int32),
            pltpu.SMEM((16,), jnp.int32),
            dma((5,)),
            dma((9,)), dma((8, 2)), dma((8,)), dma((8,)),
            dma((9,)), dma((8, 2)), dma((9,)), dma((8, 2)),
            dma((8, 3)), dma((8, 2)), dma((8,)),
            dma((8,)), dma((8,)),
            dma((8, 3)), dma((8, 2)), dma((8,)),
            dma((8,)), dma((8,)), dma((8,)), dma((8,)),
        ],
        compiler_params=pltpu.CompilerParams(
            collective_id=0, has_side_effects=True, vmem_limit_bytes=60 * 2**20
        ),
        name="affinities",
    )(embeddings, twice, features, aux, block_list, list_pairs)


def solution(mesh):
    return jax.shard_map(
        shards,
        mesh=mesh,
        in_specs=(P(("row", "col"), None), P(("row", "col")), P(("row", "col"), None), P(), P()),
        out_specs=P(("row", "col"), None),
        check_vma=False,
    )
```

```python
import math

import jax
import jax.numpy as jnp
from jax import lax
from jax.experimental import pallas as pl
from jax.experimental.pallas import tpu as pltpu
from jax.sharding import PartitionSpec as P

BLK = 128
F32 = jnp.float32
BF16 = jnp.bfloat16
LOG2E = math.log2(math.e)
INF = float("inf")
MESH = pl.DeviceIdType.MESH

PLACES = ((0, 0), (1, 0), (0, 1), (0, 3), (1, 1), (1, 3), (0, 2), (1, 2))
SLOT = {p: s for s, p in enumerate(PLACES)}
BACK = [SLOT[(dx, (4 - e) % 4)] for dx, e in PLACES]
RECTS = ((0, 2, 0, 2), (2, 1, 0, 2), (0, 3, 2, 1), (3, 1, 0, 3), (0, 4, 3, 1))


def pick(i, values):
    return sum((i == s).astype(jnp.int32) * v for s, v in enumerate(values) if v)


def kernel(
    x_ref, f_ref, rate_ref, bl_ref, lp_ref, out_ref,
    rx, cx, fb, t_ref, rn, rc, ra, ca, cs, tr, al, ral, cal, cv, w0, w1, mn, sr, ob, obr, rl, cl,
    loc, rx_s, rx_r, dd_s, dd_r, cx_s, cx_r, fb_s, fb_r, tr_s, tr_r,
    al_s, ral_r, cal_r, sr_s, sr_r, ob_s, ob_r,
):
    own, wide = x_ref.shape
    feats = f_ref.shape[1]
    every = 8 * own
    row = lax.axis_index("row")
    col = lax.axis_index("col")
    xl, y, core = col // 8, (col // 2) % 4, col % 2
    z, xh = row // 2, row % 2

    def rpeer(dx, dy, dk):
        return {"col": ((xl + dx) % 2) * 8 + ((y + dy + 4) % 4) * 2 + (core + dk) % 2}

    def cpeer(dx, dz):
        return {
            "row": ((z + dz + 4) % 4) * 2 + (xh + dx) % 2,
            "col": ((xl + dx) % 2) * 8 + y * 2 + core,
        }

    barrier = pltpu.get_barrier_semaphore()
    met = [rpeer(0, 0, 1), rpeer(1, 0, 0), rpeer(0, 1, 0), rpeer(0, -1, 0)]
    met += [cpeer(1, 0), cpeer(0, 1), cpeer(0, -1)]
    for to in met:
        pl.semaphore_signal(barrier, inc=1, device_id=to, device_id_type=MESH)

    locals_ = [
        pltpu.make_async_copy(x_ref, rx.at[0, 0], loc.at[0]),
        pltpu.make_async_copy(x_ref, cx.at[0], loc.at[1]),
        pltpu.make_async_copy(f_ref, fb.at[0], loc.at[2]),
    ]
    for c in locals_:
        c.start()

    for i, (dx, e) in enumerate(PLACES):
        for h in range(2):
            owner = row * 16 + rpeer(dx, -e, h)["col"]
            for b in range(2):
                rl[i * 4 + h * 2 + b] = bl_ref[owner * 2 + b]
        owner = cpeer(dx, -e)["row"] * 16 + cpeer(dx, -e)["col"]
        for b in range(2):
            cl[i * 2 + b] = bl_ref[owner * 2 + b]
    cs[...] = jnp.zeros_like(cs)
    w0[...] = jnp.zeros_like(w0)

    for c in locals_:
        c.wait()
    xf = rx[0, 0].astype(F32)
    norm = jnp.sum(xf * xf, axis=1, keepdims=True) * 0.5
    norm = jnp.transpose(jnp.broadcast_to(norm, (own, 128)))
    ra[0, 0, 0:1, :] = norm[0:1, :]
    ra[0, 0, 1:8, :] = rate_ref[1:8, :]
    ca[0] = ra[0, 0]

    pl.semaphore_wait(barrier, len(met))

    started = []

    def remote(src, dst, ssem, rsem, to):
        return pltpu.make_async_remote_copy(
            src_ref=src, dst_ref=dst, send_sem=ssem, recv_sem=rsem, device_id=to, device_id_type=MESH
        )

    def send(make):
        remote(*make()).start()
        started.append(make)

    def arrived(dst, rsem):
        remote(dst, dst, rsem, rsem, rpeer(0, 0, 1)).wait_recv()

    class Gather:
        def __init__(self, view, side, ssem, rsem, peer, size):
            self.view, self.side, self.peer, self.size = view, side, peer, size
            self.ssem, self.rsem = ssem, rsem

        def move(self, m, a, b, part, to):
            n = self.size if part is None else self.size // 2
            lo = self.size // 2 if part == 1 else 0
            send(lambda: (self.view(a, lo, n), self.view(b, lo, n), self.ssem.at[m, 0], self.rsem.at[b, part or 0], self.peer(*to)))
            if self.side is not None and part != 1:
                send(lambda: (self.side(a), self.side(b), self.ssem.at[m, 1], self.rsem.at[b, 2], self.peer(*to)))

        def own_x(self):
            self.move(0, 0, 1, None, (1, 0))

        def ring(self, dx):
            base = SLOT[(dx, 0)]
            self.move(1 + 4 * dx, base, SLOT[(dx, 1)], None, (0, 1))
            self.move(2 + 4 * dx, base, SLOT[(dx, 3)], None, (0, -1))

        def halves(self, dx):
            self.move(3 + 4 * dx, SLOT[(dx, 1)], SLOT[(dx, 2)], 0, (0, 1))
            self.move(4 + 4 * dx, SLOT[(dx, 3)], SLOT[(dx, 2)], 1, (0, -1))

        def recv(self, slot):
            if PLACES[slot][1] == 2:
                n = self.size // 2
                arrived(self.view(slot, 0, n), self.rsem.at[slot, 0])
                arrived(self.view(slot, n, n), self.rsem.at[slot, 1])
            else:
                arrived(self.view(slot, 0, self.size), self.rsem.at[slot, 0])
            if self.side is not None:
                arrived(self.side(slot), self.rsem.at[slot, 2])

    rows = Gather(lambda s, lo, n: rx.at[s, 0, pl.ds(lo, n)], lambda s: ra.at[s, 0], rx_s, rx_r, lambda dx, d: rpeer(dx, d, 0), own)
    cols = Gather(lambda s, lo, n: cx.at[s, pl.ds(lo, n)], lambda s: ca.at[s], cx_s, cx_r, cpeer, own)
    feat = Gather(lambda s, lo, n: fb.at[s, pl.ds(lo, n)], None, fb_s, fb_r, cpeer, own)

    def sibling(slot):
        send(lambda: (rx.at[slot, 0], rx.at[slot, 1], dd_s.at[slot, 0], dd_r.at[slot, 0], rpeer(0, 0, 1)))
        send(lambda: (ra.at[slot, 0], ra.at[slot, 1], dd_s.at[slot, 1], dd_r.at[slot, 1], rpeer(0, 0, 1)))

    def lanes(a8, k):
        return jnp.broadcast_to(jnp.transpose(a8)[:, k : k + 1], (own, 128))

    def row_terms(i, h):
        rn[i, h * own : (h + 1) * own, :] = lanes(ra[i, h], 0)
        rc[i, h * own : (h + 1) * own, :] = lanes(ra[i, h], 1)

    def row_ready(i):
        row_terms(i, 0)
        arrived(rx.at[i, 1], dd_r.at[i, 0])
        arrived(ra.at[i, 1], dd_r.at[i, 1])
        row_terms(i, 1)

    def pair(ri, qi):
        m, n = 4 * own, 2 * own
        lhs = rx[pl.ds(2 * ri, 2)].reshape(m, wide)
        rhs = cx[pl.ds(2 * qi, 2)].reshape(n, wide)
        s = lax.dot_general(lhs, rhs, (((1,), (1,)), ((), ())), preferred_element_type=F32)
        self_pen = jnp.where(ri + qi == 0, INF, 0.0).astype(F32)
        acc = [jnp.zeros((8, BLK), F32) for _ in range(n // BLK)]
        per = own // BLK
        for b in range(m // BLK):
            base = []
            for cb in range(n // BLK):
                on = lp_ref[rl[ri * (m // BLK) + b], cl[qi * (n // BLK) + cb]]
                pen = jnp.where(on > 0, 0.0, INF).astype(F32)
                base.append(ca[2 * qi + cb // per, 0:1, (cb % per) * BLK : (cb % per + 1) * BLK] + pen)
            for r8 in range(BLK // 8):
                lo = b * BLK + r8 * 8
                at = (2 * ri + lo // (2 * own), slice(lo % (2 * own), lo % (2 * own) + 8))
                r_n = rn[at[0], at[1], :]
                for cb in range(n // BLK):
                    d = (r_n + base[cb]) - s[lo : lo + 8, cb * BLK : (cb + 1) * BLK]
                    if b == cb and b < per:
                        at_r = r8 * 8 + lax.broadcasted_iota(jnp.int32, (8, BLK), 0)
                        at_c = lax.broadcasted_iota(jnp.int32, (8, BLK), 1)
                        d = d + jnp.where(at_r == at_c, self_pen, 0.0)
                    t_ref[at[0], at[1], pl.ds(pl.multiple_of(qi * n + cb * BLK, BLK), BLK)] = d
                    rate = ca[2 * qi + cb // per, 1:2, (cb % per) * BLK : (cb % per + 1) * BLK]
                    acc[cb] = acc[cb] + jnp.exp2(d * rate)
        for c in range(2):
            cs[2 * qi + c] = cs[2 * qi + c] + jnp.concatenate(acc[c * per : (c + 1) * per], axis=1)

    def give_sum(q):
        dx, e = PLACES[q]
        send(lambda: (cs.at[q], tr.at[BACK[q]], tr_s.at[q], tr_r.at[BACK[q]], cpeer(dx, -e)))

    rows.ring(0)
    cols.ring(0)
    rows.own_x()
    cols.own_x()
    sibling(0)
    row_ready(0)

    def before(k):
        if k == 0:
            for g in (rows, cols):
                g.recv(1)
                g.ring(1)
                g.recv(2)
                g.recv(3)
                g.halves(0)
            for s in (1, 2, 3):
                sibling(s)
            for s in (1, 2, 3):
                row_ready(s)
        if k == 1:
            for g in (rows, cols):
                g.recv(4)
                g.recv(5)
                g.halves(1)
            for s in (4, 5):
                sibling(s)
            feat.ring(0)
            feat.own_x()
            for s in (4, 5):
                row_ready(s)
        if k == 3:
            for s in (6, 7):
                rows.recv(s)
                sibling(s)
            for s in (6, 7):
                row_ready(s)
        if k == 4:
            for s in (6, 7):
                cols.recv(s)
            for q in range(1, 6):
                give_sum(q)
            feat.recv(1)
            feat.ring(1)
            feat.recv(2)
            feat.recv(3)
            feat.halves(0)

    def rect(k, carry):
        first, count_r, lead, count_c = (pick(k, [r[f] for r in RECTS]) for f in range(4))
        for j in (0, 1, 3, 4):
            @pl.when(k == j)
            def _():
                before(j)

        def inner_c(cc, carry2):
            def inner_r(rr, carry3):
                pair(first + rr, lead + cc)
                return carry3

            return lax.fori_loop(0, count_r, inner_r, carry2)

        return lax.fori_loop(0, count_c, inner_c, carry)

    lax.fori_loop(0, len(RECTS), rect, 0)

    give_sum(6)
    give_sum(7)
    feat.recv(4)
    feat.recv(5)
    feat.halves(1)
    total = cs[0]
    for q in range(1, 8):
        arrived(tr.at[q], tr_r.at[q])
        total = total + tr[q]
    al[...] = jnp.broadcast_to(0.5 / jnp.sum(total, axis=0, keepdims=True), al.shape)
    ral[0, 0] = al[...]
    cal[0] = al[...]
    for i in (7, 6, 5, 4, 1, 3, 2, 0):
        dx, e = PLACES[i]
        if i > 0:
            send(lambda i=i, dx=dx, e=e: (al, cal.at[i], al_s.at[i, 2], cal_r.at[i], cpeer(dx, e)))
    for i in (7, 6, 5, 4, 1, 3, 2, 0):
        dx, e = PLACES[i]
        for h in (1, 0):
            if i + h > 0:
                send(lambda i=i, h=h, dx=dx, e=e: (al, ral.at[i, h], al_s.at[i, h], ral_r.at[i, h], rpeer(dx, e, h)))
    for q in range(8):
        if q > 0:
            arrived(cal.at[q], cal_r.at[q])
        cv[0:1, q * own : (q + 1) * own] = ca[q, 1:2, :]
        cv[1:2, q * own : (q + 1) * own] = cal[q, 0:1, :]

    feat.recv(6)
    feat.recv(7)
    step_r, step_c = 64, 256

    def weigh(i, h, w_ref):
        ar = jnp.transpose(ral[i, h])[:, 0:1]
        for r in range(own // step_r):
            a_r = jnp.broadcast_to(ar[r * step_r : (r + 1) * step_r], (step_r, 128))
            a_r = jnp.concatenate([a_r] * (step_c // 128), axis=1)
            c_r = rc[i, h * own + r * step_r : h * own + (r + 1) * step_r, :]
            c_r = jnp.concatenate([c_r] * (step_c // 128), axis=1)
            for c in range(every // step_c):
                sl = slice(c * step_c, (c + 1) * step_c)
                d = t_ref[i, h * own + r * step_r : h * own + (r + 1) * step_r, sl]
                v = jnp.exp2(d * c_r) * a_r + jnp.exp2(d * cv[0:1, sl]) * cv[1:2, sl]
                w_ref[r * step_r : (r + 1) * step_r, sl] = v.astype(BF16)

    def order(j):
        return 7 - j - 2 * (j == 4).astype(jnp.int32) + ((j == 5) | (j == 6)).astype(jnp.int32)

    def to_sibling(i):
        return remote(
            t_ref.at[i, pl.ds(own, own), pl.ds(0, feats)], sr.at[i], sr_s.at[i], sr_r.at[i], rpeer(0, 0, 1)
        )

    def to_owner(i):
        dx, e = pick(i, [p[0] for p in PLACES]), pick(i, [p[1] for p in PLACES])
        b = pick(i, BACK)
        return remote(ob.at[i], obr.at[b], ob_s.at[i], ob_r.at[b], rpeer(dx, 4 - e, 0))

    def finish(j):
        i = order(j)
        arrived(sr.at[i], sr_r.at[i])
        ob[i] = (sr[i] + mn[j % 2]).astype(BF16)
        to_owner(i).start()

    def out_step(j, carry):
        i = order(j)
        for h in (1, 0):
            @pl.when(i + h > 0)
            def _():
                arrived(ral.at[i, h], ral_r.at[i, h])
        everything = fb[...].reshape(every, feats)
        weigh(i, 1, w1)
        mn[(j + 1) % 2] = jnp.dot(w0[...], everything, preferred_element_type=F32)

        @pl.when(j >= 2)
        def _():
            finish(j - 2)

        other = jnp.dot(w1[...], everything, preferred_element_type=F32)
        weigh(i, 0, w0)
        t_ref[i, own : 2 * own, 0:feats] = other
        to_sibling(i).start()
        return carry

    lax.fori_loop(0, 8, out_step, 0)
    finish(jnp.int32(6) + row * 0)
    result = jnp.dot(w0[...], fb[...].reshape(every, feats), preferred_element_type=F32)
    arrived(sr.at[0], sr_r.at[0])
    result = result + sr[0]
    for i in (7, 6, 5, 4, 1, 3, 2):
        arrived(obr.at[i], ob_r.at[i])
        result = result + obr[i].astype(F32)
    out_ref[...] = result
    for make in started:
        remote(*make()).wait_send()

    def drain(i, carry):
        to_sibling(i).wait_send()

        @pl.when(i > 0)
        def _():
            to_owner(i).wait_send()
        return carry

    lax.fori_loop(0, 8, drain, 0)


def shards(embeddings, spread, features, block_list, list_pairs):
    own, wide = embeddings.shape
    feats = features.shape[1]
    rate = jnp.broadcast_to(spread.astype(F32)[None] * (-2.0 * LOG2E), (8, own))
    anywhere = pl.BlockSpec(memory_space=pl.ANY)
    scalars = pl.BlockSpec(memory_space=pltpu.SMEM)
    whole = pl.BlockSpec(memory_space=pltpu.VMEM)
    vmem, dma = pltpu.VMEM, pltpu.SemaphoreType.DMA
    return pl.pallas_call(
        kernel,
        out_shape=jax.ShapeDtypeStruct((own, feats), F32),
        in_specs=[anywhere] * 2 + [whole] + [scalars] * 2,
        out_specs=whole,
        scratch_shapes=[
            vmem((8, 2, own, wide), BF16),
            vmem((8, own, wide), BF16),
            vmem((8, own, feats), BF16),
            vmem((8, 2 * own, 8 * own), F32),
            vmem((8, 2 * own, 128), F32),
            vmem((8, 2 * own, 128), F32),
            vmem((8, 2, 8, own), F32),
            vmem((8, 8, own), F32),
            vmem((8, 8, own), F32),
            vmem((8, 8, own), F32),
            vmem((8, own), F32),
            vmem((8, 2, 8, own), F32),
            vmem((8, 8, own), F32),
            vmem((8, 8 * own), F32),
            vmem((own, 8 * own), BF16),
            vmem((own, 8 * own), BF16),
            vmem((2, own, feats), F32),
            vmem((8, own, feats), F32),
            vmem((8, own, feats), BF16),
            vmem((8, own, feats), BF16),
            pltpu.SMEM((32,), jnp.int32),
            pltpu.SMEM((16,), jnp.int32),
            dma((3,)),
            dma((9, 2)), dma((8, 3)), dma((8, 2)), dma((8, 2)),
            dma((9, 2)), dma((8, 3)), dma((9, 2)), dma((8, 3)),
            dma((8,)), dma((8,)),
            dma((8, 3)), dma((8, 2)), dma((8,)),
            dma((8,)), dma((8,)), dma((8,)), dma((8,)),
        ],
        compiler_params=pltpu.CompilerParams(
            collective_id=0, has_side_effects=True, vmem_limit_bytes=61 * 2**20
        ),
        name="affinities",
    )(embeddings, features, rate, block_list, list_pairs)


def solution(mesh):
    return jax.shard_map(
        shards,
        mesh=mesh,
        in_specs=(P(("row", "col"), None), P(("row", "col")), P(("row", "col"), None), P(), P()),
        out_specs=P(("row", "col"), None),
        check_vma=False,
    )
```

```python
import math

import jax
import jax.numpy as jnp
from jax import lax
from jax.experimental import pallas as pl
from jax.experimental.pallas import tpu as pltpu
from jax.sharding import PartitionSpec as P

BLK = 128
F32 = jnp.float32
BF16 = jnp.bfloat16
LOG2E = math.log2(math.e)
INF = float("inf")
MESH = pl.DeviceIdType.MESH

PLACES = ((0, 0), (1, 0), (0, 1), (0, 3), (0, 2), (1, 1), (1, 3), (1, 2))
SLOT = {p: s for s, p in enumerate(PLACES)}
ORDER = (0, 7, 4, 5, 6, 1, 3, 2)
BACK = [SLOT[(dx, (4 - e) % 4)] for dx, e in PLACES]
RECTS = ((0, 2, 0, 2), (2, 1, 0, 2), (0, 3, 2, 1), (3, 1, 0, 3), (0, 4, 3, 1))


def pick(i, values):
    return sum((i == s).astype(jnp.int32) * v for s, v in enumerate(values) if v)


def kernel(
    x_ref, f_ref, rate_ref, bl_ref, lp_ref, out_ref,
    rx, cx, fb, t_ref, rn, rc, ra, ca, cs, tr, al, ral, cm, cv, w0, mn, sr, ob, obr, rl, cl,
    loc, rx_s, rx_r, dd_s, dd_r, cx_s, cx_r, fb_s, fb_r, tr_s, tr_r,
    al_s, ral_r, sr_s, sr_r, ob_s, ob_r,
):
    own, wide = x_ref.shape
    feats = f_ref.shape[1]
    every = 8 * own
    row = lax.axis_index("row")
    col = lax.axis_index("col")
    xl, y, core = col // 8, (col // 2) % 4, col % 2
    z, xh = row // 2, row % 2

    def rpeer(dx, dy, dk):
        return {"col": ((xl + dx) % 2) * 8 + ((y + dy + 4) % 4) * 2 + (core + dk) % 2}

    def cpeer(dx, dz):
        return {
            "row": ((z + dz + 4) % 4) * 2 + (xh + dx) % 2,
            "col": ((xl + dx) % 2) * 8 + y * 2 + core,
        }

    barrier = pltpu.get_barrier_semaphore()
    met = [rpeer(0, 0, 1), rpeer(1, 0, 0), rpeer(0, 1, 0), rpeer(0, -1, 0)]
    met += [cpeer(1, 0), cpeer(0, 1), cpeer(0, -1)]
    for to in met:
        pl.semaphore_signal(barrier, inc=1, device_id=to, device_id_type=MESH)

    locals_ = [
        pltpu.make_async_copy(x_ref, rx.at[0, 0], loc.at[0]),
        pltpu.make_async_copy(x_ref, cx.at[0], loc.at[1]),
        pltpu.make_async_copy(f_ref, fb.at[0], loc.at[2]),
    ]
    for c in locals_:
        c.start()

    for i, (dx, e) in enumerate(PLACES):
        for h in range(2):
            owner = row * 16 + rpeer(dx, -e, h)["col"]
            for b in range(2):
                rl[i * 4 + h * 2 + b] = bl_ref[owner * 2 + b]
        owner = cpeer(dx, -e)["row"] * 16 + cpeer(dx, -e)["col"]
        for b in range(2):
            cl[i * 2 + b] = bl_ref[owner * 2 + b]
    cs[...] = jnp.zeros_like(cs)

    for c in locals_:
        c.wait()
    xf = rx[0, 0].astype(F32)
    norm = jnp.sum(xf * xf, axis=1, keepdims=True) * 0.5
    norm = jnp.transpose(jnp.broadcast_to(norm, (own, 128)))
    ra[0, 0, 0:1, :] = norm[0:1, :]
    ra[0, 0, 1:8, :] = rate_ref[1:8, :]
    ca[0] = ra[0, 0]

    pl.semaphore_wait(barrier, len(met))

    started = []

    def remote(src, dst, ssem, rsem, to):
        return pltpu.make_async_remote_copy(
            src_ref=src, dst_ref=dst, send_sem=ssem, recv_sem=rsem, device_id=to, device_id_type=MESH
        )

    def send(make):
        remote(*make()).start()
        started.append(make)

    def arrived(dst, rsem):
        remote(dst, dst, rsem, rsem, rpeer(0, 0, 1)).wait_recv()

    class Gather:
        def __init__(self, view, side, ssem, rsem, peer, size):
            self.view, self.side, self.peer, self.size = view, side, peer, size
            self.ssem, self.rsem = ssem, rsem

        def move(self, m, a, b, part, to):
            n = self.size if part is None else self.size // 2
            lo = self.size // 2 if part == 1 else 0
            send(lambda: (self.view(a, lo, n), self.view(b, lo, n), self.ssem.at[m, 0], self.rsem.at[b, part or 0], self.peer(*to)))
            if self.side is not None and part != 1:
                send(lambda: (self.side(a), self.side(b), self.ssem.at[m, 1], self.rsem.at[b, 2], self.peer(*to)))

        def first(self):
            self.move(1, 0, SLOT[(0, 1)], None, (0, 1))
            self.move(2, 0, SLOT[(0, 3)], None, (0, -1))
            self.move(0, 0, SLOT[(1, 0)], None, (1, 0))

        def second(self):
            self.recv(SLOT[(0, 1)])
            self.recv(SLOT[(0, 3)])
            self.move(3, SLOT[(0, 1)], SLOT[(0, 2)], 0, (0, 1))
            self.move(4, SLOT[(0, 3)], SLOT[(0, 2)], 1, (0, -1))
            self.move(6, SLOT[(0, 1)], SLOT[(1, 1)], None, (1, 0))
            self.recv(SLOT[(1, 0)])
            self.move(5, SLOT[(1, 0)], SLOT[(1, 3)], None, (0, -1))

        def third(self):
            self.recv(SLOT[(0, 2)])
            self.move(7, SLOT[(0, 2)], SLOT[(1, 2)], 0, (1, 0))

        def fourth(self):
            self.recv(SLOT[(1, 1)])
            self.move(8, SLOT[(1, 1)], SLOT[(1, 2)], 1, (0, 1))

        def last(self):
            self.recv(SLOT[(1, 3)])
            self.recv(SLOT[(1, 2)])

        def recv(self, slot):
            if PLACES[slot][1] == 2:
                n = self.size // 2
                arrived(self.view(slot, 0, n), self.rsem.at[slot, 0])
                arrived(self.view(slot, n, n), self.rsem.at[slot, 1])
            else:
                arrived(self.view(slot, 0, self.size), self.rsem.at[slot, 0])
            if self.side is not None:
                arrived(self.side(slot), self.rsem.at[slot, 2])

    rows = Gather(lambda s, lo, n: rx.at[s, 0, pl.ds(lo, n)], lambda s: ra.at[s, 0], rx_s, rx_r, lambda dx, d: rpeer(dx, d, 0), own)
    cols = Gather(lambda s, lo, n: cx.at[s, pl.ds(lo, n)], lambda s: ca.at[s], cx_s, cx_r, cpeer, own)
    feat = Gather(lambda s, lo, n: fb.at[s, pl.ds(lo, n)], None, fb_s, fb_r, cpeer, own)

    def sibling(slot):
        send(lambda: (rx.at[slot, 0], rx.at[slot, 1], dd_s.at[slot, 0], dd_r.at[slot, 0], rpeer(0, 0, 1)))
        send(lambda: (ra.at[slot, 0], ra.at[slot, 1], dd_s.at[slot, 1], dd_r.at[slot, 1], rpeer(0, 0, 1)))

    def lanes(a8, k):
        return jnp.broadcast_to(jnp.transpose(a8)[:, k : k + 1], (own, 128))

    def row_terms(i, h):
        rn[i, h * own : (h + 1) * own, :] = lanes(ra[i, h], 0)
        rc[i, h * own : (h + 1) * own, :] = lanes(ra[i, h], 1)

    def row_ready(i):
        row_terms(i, 0)
        arrived(rx.at[i, 1], dd_r.at[i, 0])
        arrived(ra.at[i, 1], dd_r.at[i, 1])
        row_terms(i, 1)

    def pair(ri, qi):
        m, n = 4 * own, 2 * own
        lhs = rx[pl.ds(2 * ri, 2)].reshape(m, wide)
        rhs = cx[pl.ds(2 * qi, 2)].reshape(n, wide)
        s = lax.dot_general(lhs, rhs, (((1,), (1,)), ((), ())), preferred_element_type=F32)
        self_pen = jnp.where(ri + qi == 0, INF, 0.0).astype(F32)
        acc = [jnp.zeros((8, BLK), F32) for _ in range(n // BLK)]
        per = own // BLK
        for b in range(m // BLK):
            base = []
            for cb in range(n // BLK):
                on = lp_ref[rl[ri * (m // BLK) + b], cl[qi * (n // BLK) + cb]]
                pen = jnp.where(on > 0, 0.0, INF).astype(F32)
                base.append(ca[2 * qi + cb // per, 0:1, (cb % per) * BLK : (cb % per + 1) * BLK] + pen)
            for r8 in range(BLK // 8):
                lo = b * BLK + r8 * 8
                at = (2 * ri + lo // (2 * own), slice(lo % (2 * own), lo % (2 * own) + 8))
                r_n = rn[at[0], at[1], :]
                for cb in range(n // BLK):
                    d = (r_n + base[cb]) - s[lo : lo + 8, cb * BLK : (cb + 1) * BLK]
                    if b == cb and b < per:
                        at_r = r8 * 8 + lax.broadcasted_iota(jnp.int32, (8, BLK), 0)
                        at_c = lax.broadcasted_iota(jnp.int32, (8, BLK), 1)
                        d = d + jnp.where(at_r == at_c, self_pen, 0.0)
                    t_ref[at[0], at[1], pl.ds(pl.multiple_of(qi * n + cb * BLK, BLK), BLK)] = d
                    rate = ca[2 * qi + cb // per, 1:2, (cb % per) * BLK : (cb % per + 1) * BLK]
                    acc[cb] = acc[cb] + jnp.exp2(d * rate)
        for c in range(2):
            cs[2 * qi + c] = cs[2 * qi + c] + jnp.concatenate(acc[c * per : (c + 1) * per], axis=1)

    rows.first()
    cols.first()
    sibling(0)
    row_ready(0)

    def before(k):
        if k == 0:
            rows.second()
            cols.second()
            for s in (1, 2, 3):
                sibling(s)
            for s in (1, 2, 3):
                row_ready(s)
        if k == 1:
            rows.third()
            cols.third()
            rows.fourth()
            cols.fourth()
            feat.first()
            for s in (4, 5):
                sibling(s)
            for s in (4, 5):
                row_ready(s)
        if k == 3:
            rows.last()
            for s in (6, 7):
                sibling(s)
            cols.last()
            for s in (6, 7):
                row_ready(s)
        if k == 4:
            feat.second()

    def rect(k, carry):
        first, count_r, lead, count_c = (pick(k, [r[f] for r in RECTS]) for f in range(4))
        for j in (0, 1, 3, 4):
            @pl.when(k == j)
            def _():
                before(j)

        def inner_c(cc, carry2):
            def inner_r(rr, carry3):
                pair(first + rr, lead + cc)
                return carry3

            return lax.fori_loop(0, count_r, inner_r, carry2)

        return lax.fori_loop(0, count_c, inner_c, carry)

    lax.fori_loop(0, len(RECTS), rect, 0)

    for q in range(8):
        cm[q : q + 1, :] = jnp.sum(cs[q], axis=0, keepdims=True)
    for s in range(1, 8):
        dx, e = PLACES[s]
        send(lambda s=s, dx=dx, e=e: (cm, tr.at[s], tr_s.at[s], tr_r.at[s], cpeer(dx, e)))
    feat.third()
    feat.fourth()
    for s in range(1, 8):
        arrived(tr.at[s], tr_r.at[s])

    def factor(q):
        total = cm[q : q + 1, :]
        for s in range(1, 8):
            p = SLOT[((PLACES[q][0] + PLACES[s][0]) % 2, (PLACES[q][1] - PLACES[s][1]) % 4)]
            total = total + tr[s, p : p + 1, :]
        return 0.5 / total

    al[...] = jnp.broadcast_to(factor(0), al.shape)
    ral[0, 0] = al[...]
    for i in ORDER:
        dx, e = PLACES[i]
        for h in (1, 0):
            if i + h > 0:
                send(lambda i=i, h=h, dx=dx, e=e: (al, ral.at[i, h], al_s.at[i, h], ral_r.at[i, h], rpeer(dx, e, h)))
    for q in range(8):
        cv[0:1, q * own : (q + 1) * own] = ca[q, 1:2, :]
        cv[1:2, q * own : (q + 1) * own] = al[0:1, :] if q == 0 else factor(q)
    feat.last()
    step_r, step_c = 64, 256

    def weigh(i, w_ref):
        for r in range(2 * own // step_r):
            if r * step_r % own == 0:
                ar = jnp.transpose(ral[i, r * step_r // own])[:, 0:1]
            lo = r * step_r % own
            a_r = jnp.broadcast_to(ar[lo : lo + step_r], (step_r, 128))
            a_r = jnp.concatenate([a_r] * (step_c // 128), axis=1)
            at = slice(r * step_r, (r + 1) * step_r)
            c_r = jnp.concatenate([rc[i, at, :]] * (step_c // 128), axis=1)
            for c in range(every // step_c):
                sl = slice(c * step_c, (c + 1) * step_c)
                d = t_ref[i, at, sl]
                v = jnp.exp2(d * c_r) * a_r + jnp.exp2(d * cv[0:1, sl]) * cv[1:2, sl]
                w_ref[at, sl] = v.astype(BF16)

    def order(j):
        return pick(j, ORDER)

    def to_sibling(i):
        return remote(
            t_ref.at[i, pl.ds(own, own), pl.ds(0, feats)], sr.at[i], sr_s.at[i], sr_r.at[i], rpeer(0, 0, 1)
        )

    def to_owner(i):
        dx, e = pick(i, [p[0] for p in PLACES]), pick(i, [p[1] for p in PLACES])
        b = pick(i, BACK)
        return remote(ob.at[i], obr.at[b], ob_s.at[i], ob_r.at[b], rpeer(dx, 4 - e, 0))

    def give_sibling(i, part):
        t_ref[i, own : 2 * own, 0:feats] = part
        to_sibling(i).start()

    def finish(j):
        i = order(j)
        arrived(sr.at[i], sr_r.at[i])
        ob[i] = (sr[i] + mn[j % 2]).astype(BF16)
        to_owner(i).start()

    def await_factors(i):
        for h in range(2):
            @pl.when(i + h > 0)
            def _():
                arrived(ral.at[i, h], ral_r.at[i, h])

    def multiply(w_ref):
        return jnp.dot(w_ref[...], fb[...].reshape(every, feats), preferred_element_type=F32)

    def hand_out(j, part):
        i = order(j)
        give_sibling(i, part[own:])
        mn[j % 2] = part[:own]

        @pl.when(j == 0)
        def _():
            t_ref[0, 0:own, 0:feats] = part[:own]

        @pl.when(j > 1)
        def _():
            finish(j - 1)

    def out_step(j, carry):
        i = order(j)
        await_factors(i)
        weigh(i, w0)
        hand_out(j, multiply(w0))
        return carry

    lax.fori_loop(0, 8, out_step, 0)
    finish(row * 0 + 7)
    result = t_ref[0, 0:own, 0:feats]
    arrived(sr.at[0], sr_r.at[0])
    result = result + sr[0]
    for i in ORDER[1:]:
        arrived(obr.at[i], ob_r.at[i])
        result = result + obr[i].astype(F32)
    out_ref[...] = result
    for make in started:
        remote(*make()).wait_send()

    def drain(i, carry):
        to_sibling(i).wait_send()

        @pl.when(i > 0)
        def _():
            to_owner(i).wait_send()
        return carry

    lax.fori_loop(0, 8, drain, 0)


def shards(embeddings, spread, features, block_list, list_pairs):
    own, wide = embeddings.shape
    feats = features.shape[1]
    rate = jnp.broadcast_to(spread.astype(F32)[None] * (-2.0 * LOG2E), (8, own))
    anywhere = pl.BlockSpec(memory_space=pl.ANY)
    scalars = pl.BlockSpec(memory_space=pltpu.SMEM)
    whole = pl.BlockSpec(memory_space=pltpu.VMEM)
    vmem, dma = pltpu.VMEM, pltpu.SemaphoreType.DMA
    return pl.pallas_call(
        kernel,
        out_shape=jax.ShapeDtypeStruct((own, feats), F32),
        in_specs=[anywhere] * 2 + [whole] + [scalars] * 2,
        out_specs=whole,
        scratch_shapes=[
            vmem((8, 2, own, wide), BF16),
            vmem((8, own, wide), BF16),
            vmem((8, own, feats), BF16),
            vmem((8, 2 * own, 8 * own), F32),
            vmem((8, 2 * own, 128), F32),
            vmem((8, 2 * own, 128), F32),
            vmem((8, 2, 8, own), F32),
            vmem((8, 8, own), F32),
            vmem((8, 8, own), F32),
            vmem((8, 8, own), F32),
            vmem((8, own), F32),
            vmem((8, 2, 8, own), F32),
            vmem((8, own), F32),
            vmem((8, 8 * own), F32),
            vmem((2 * own, 8 * own), BF16),
            vmem((2, own, feats), F32),
            vmem((8, own, feats), F32),
            vmem((8, own, feats), BF16),
            vmem((8, own, feats), BF16),
            pltpu.SMEM((32,), jnp.int32),
            pltpu.SMEM((16,), jnp.int32),
            dma((3,)),
            dma((9, 2)), dma((8, 3)), dma((8, 2)), dma((8, 2)),
            dma((9, 2)), dma((8, 3)), dma((9, 2)), dma((8, 3)),
            dma((8,)), dma((8,)),
            dma((8, 2)), dma((8, 2)),
            dma((8,)), dma((8,)), dma((8,)), dma((8,)),
        ],
        compiler_params=pltpu.CompilerParams(
            collective_id=0, has_side_effects=True, vmem_limit_bytes=61 * 2**20
        ),
        name="affinities",
    )(embeddings, features, rate, block_list, list_pairs)


def solution(mesh):
    return jax.shard_map(
        shards,
        mesh=mesh,
        in_specs=(P(("row", "col"), None), P(("row", "col")), P(("row", "col"), None), P(), P()),
        out_specs=P(("row", "col"), None),
        check_vma=False,
    )
```

```python
import math

import jax
import jax.numpy as jnp
from jax import lax
from jax.experimental import pallas as pl
from jax.experimental.pallas import tpu as pltpu
from jax.sharding import PartitionSpec as P

BLK = 128
F32 = jnp.float32
BF16 = jnp.bfloat16
LOG2E = math.log2(math.e)
INF = float("inf")
MESH = pl.DeviceIdType.MESH

PLACES = ((0, 0), (1, 0), (0, 1), (0, 3), (0, 2), (1, 1), (1, 3), (1, 2))
SLOT = {p: s for s, p in enumerate(PLACES)}
ORDER = (0, 4, 7, 6, 5, 1, 2, 3)
BACK = [SLOT[(dx, (4 - e) % 4)] for dx, e in PLACES]
RECTS = ((0, 2, 0, 2), (2, 1, 0, 2), (0, 3, 2, 1), (3, 1, 0, 3), (0, 4, 3, 1))


def pick(i, values):
    return sum((i == s).astype(jnp.int32) * v for s, v in enumerate(values) if v)


def kernel(
    x_ref, f_ref, rate_ref, bl_ref, lp_ref, out_ref,
    rx, cx, fb, t_ref, rn, rc, ra, ca, cs, tr, al, ral, cm, cv, w0, mn, sr, ob, obr, rl, cl,
    loc, rx_s, rx_r, dd_s, dd_r, cx_s, cx_r, fb_s, fb_r, tr_s, tr_r,
    al_s, ral_r, sr_s, sr_r, ob_s, ob_r,
):
    own, wide = x_ref.shape
    feats = f_ref.shape[1]
    every = 8 * own
    row = lax.axis_index("row")
    col = lax.axis_index("col")
    xl, y, core = col // 8, (col // 2) % 4, col % 2
    z, xh = row // 2, row % 2

    def rpeer(dx, dy, dk):
        return {"col": ((xl + dx) % 2) * 8 + ((y + dy + 4) % 4) * 2 + (core + dk) % 2}

    def cpeer(dx, dz):
        return {
            "row": ((z + dz + 4) % 4) * 2 + (xh + dx) % 2,
            "col": ((xl + dx) % 2) * 8 + y * 2 + core,
        }

    barrier = pltpu.get_barrier_semaphore()
    met = [rpeer(0, 0, 1), rpeer(1, 0, 0), rpeer(0, 1, 0), rpeer(0, -1, 0)]
    met += [cpeer(1, 0), cpeer(0, 1), cpeer(0, -1)]
    for to in met:
        pl.semaphore_signal(barrier, inc=1, device_id=to, device_id_type=MESH)

    locals_ = [
        pltpu.make_async_copy(x_ref, rx.at[0, 0], loc.at[0]),
        pltpu.make_async_copy(x_ref, cx.at[0], loc.at[1]),
        pltpu.make_async_copy(f_ref, fb.at[0], loc.at[2]),
    ]
    for c in locals_:
        c.start()

    for i, (dx, e) in enumerate(PLACES):
        for h in range(2):
            owner = row * 16 + rpeer(dx, -e, h)["col"]
            for b in range(2):
                rl[i * 4 + h * 2 + b] = bl_ref[owner * 2 + b]
        owner = cpeer(dx, -e)["row"] * 16 + cpeer(dx, -e)["col"]
        for b in range(2):
            cl[i * 2 + b] = bl_ref[owner * 2 + b]
    cs[...] = jnp.zeros_like(cs)

    for c in locals_:
        c.wait()
    xf = rx[0, 0].astype(F32)
    norm = jnp.sum(xf * xf, axis=1, keepdims=True) * 0.5
    norm = jnp.transpose(jnp.broadcast_to(norm, (own, 128)))
    ra[0, 0, 0:1, :] = norm[0:1, :]
    rate = rate_ref[...].astype(F32).reshape(1, own) * (-2.0 * LOG2E)
    ra[0, 0, 1:8, :] = jnp.broadcast_to(rate, (7, own))
    ca[0] = ra[0, 0]

    pl.semaphore_wait(barrier, len(met))

    started = []

    def remote(src, dst, ssem, rsem, to):
        return pltpu.make_async_remote_copy(
            src_ref=src, dst_ref=dst, send_sem=ssem, recv_sem=rsem, device_id=to, device_id_type=MESH
        )

    def send(make):
        remote(*make()).start()
        started.append(make)

    def arrived(dst, rsem):
        remote(dst, dst, rsem, rsem, rpeer(0, 0, 1)).wait_recv()

    class Gather:
        def __init__(self, view, side, ssem, rsem, peer, size):
            self.view, self.side, self.peer, self.size = view, side, peer, size
            self.ssem, self.rsem = ssem, rsem

        def move(self, m, a, b, part, to):
            n = self.size if part is None else self.size // 2
            lo = self.size // 2 if part == 1 else 0
            send(lambda: (self.view(a, lo, n), self.view(b, lo, n), self.ssem.at[m, 0], self.rsem.at[b, part or 0], self.peer(*to)))
            if self.side is not None and part != 1:
                send(lambda: (self.side(a), self.side(b), self.ssem.at[m, 1], self.rsem.at[b, 2], self.peer(*to)))

        def first(self):
            self.move(1, 0, SLOT[(0, 1)], None, (0, 1))
            self.move(2, 0, SLOT[(0, 3)], None, (0, -1))
            self.move(0, 0, SLOT[(1, 0)], None, (1, 0))

        def second(self):
            self.recv(SLOT[(0, 1)])
            self.recv(SLOT[(0, 3)])
            self.move(3, SLOT[(0, 1)], SLOT[(0, 2)], 0, (0, 1))
            self.move(4, SLOT[(0, 3)], SLOT[(0, 2)], 1, (0, -1))
            self.move(6, SLOT[(0, 1)], SLOT[(1, 1)], None, (1, 0))
            self.recv(SLOT[(1, 0)])
            self.move(5, SLOT[(1, 0)], SLOT[(1, 3)], None, (0, -1))

        def third(self):
            self.recv(SLOT[(0, 2)])
            self.move(7, SLOT[(0, 2)], SLOT[(1, 2)], 0, (1, 0))

        def fourth(self):
            self.recv(SLOT[(1, 1)])
            self.move(8, SLOT[(1, 1)], SLOT[(1, 2)], 1, (0, 1))

        def last(self):
            self.recv(SLOT[(1, 3)])
            self.recv(SLOT[(1, 2)])

        def recv(self, slot):
            if PLACES[slot][1] == 2:
                n = self.size // 2
                arrived(self.view(slot, 0, n), self.rsem.at[slot, 0])
                arrived(self.view(slot, n, n), self.rsem.at[slot, 1])
            else:
                arrived(self.view(slot, 0, self.size), self.rsem.at[slot, 0])
            if self.side is not None:
                arrived(self.side(slot), self.rsem.at[slot, 2])

    rows = Gather(lambda s, lo, n: rx.at[s, 0, pl.ds(lo, n)], lambda s: ra.at[s, 0], rx_s, rx_r, lambda dx, d: rpeer(dx, d, 0), own)
    cols = Gather(lambda s, lo, n: cx.at[s, pl.ds(lo, n)], lambda s: ca.at[s], cx_s, cx_r, cpeer, own)
    feat = Gather(lambda s, lo, n: fb.at[s, pl.ds(lo, n)], None, fb_s, fb_r, cpeer, own)

    def sibling(slot):
        send(lambda: (rx.at[slot, 0], rx.at[slot, 1], dd_s.at[slot, 0], dd_r.at[slot, 0], rpeer(0, 0, 1)))
        send(lambda: (ra.at[slot, 0], ra.at[slot, 1], dd_s.at[slot, 1], dd_r.at[slot, 1], rpeer(0, 0, 1)))

    def lanes(a8, k):
        return jnp.broadcast_to(jnp.transpose(a8)[:, k : k + 1], (own, 128))

    def row_terms(i, h):
        rn[i, h * own : (h + 1) * own, :] = lanes(ra[i, h], 0)
        rc[i, h * own : (h + 1) * own, :] = lanes(ra[i, h], 1)

    def row_ready(i):
        row_terms(i, 0)
        arrived(rx.at[i, 1], dd_r.at[i, 0])
        arrived(ra.at[i, 1], dd_r.at[i, 1])
        row_terms(i, 1)

    def pair(ri, qi):
        m, n = 4 * own, 2 * own
        lhs = rx[pl.ds(2 * ri, 2)].reshape(m, wide)
        rhs = cx[pl.ds(2 * qi, 2)].reshape(n, wide)
        s = lax.dot_general(lhs, rhs, (((1,), (1,)), ((), ())), preferred_element_type=F32)
        self_pen = jnp.where(ri + qi == 0, INF, 0.0).astype(F32)
        acc = [jnp.zeros((8, BLK), F32) for _ in range(n // BLK)]
        per = own // BLK
        for b in range(m // BLK):
            base = []
            for cb in range(n // BLK):
                on = lp_ref[rl[ri * (m // BLK) + b], cl[qi * (n // BLK) + cb]]
                pen = jnp.where(on > 0, 0.0, INF).astype(F32)
                base.append(ca[2 * qi + cb // per, 0:1, (cb % per) * BLK : (cb % per + 1) * BLK] + pen)
            for r8 in range(BLK // 8):
                lo = b * BLK + r8 * 8
                at = (2 * ri + lo // (2 * own), slice(lo % (2 * own), lo % (2 * own) + 8))
                r_n = rn[at[0], at[1], :]
                for cb in range(n // BLK):
                    d = (r_n + base[cb]) - s[lo : lo + 8, cb * BLK : (cb + 1) * BLK]
                    if b == cb and b < per:
                        at_r = r8 * 8 + lax.broadcasted_iota(jnp.int32, (8, BLK), 0)
                        at_c = lax.broadcasted_iota(jnp.int32, (8, BLK), 1)
                        d = d + jnp.where(at_r == at_c, self_pen, 0.0)
                    t_ref[at[0], at[1], pl.ds(pl.multiple_of(qi * n + cb * BLK, BLK), BLK)] = d
                    rate = ca[2 * qi + cb // per, 1:2, (cb % per) * BLK : (cb % per + 1) * BLK]
                    acc[cb] = acc[cb] + jnp.exp2(d * rate)
        for c in range(2):
            cs[2 * qi + c] = cs[2 * qi + c] + jnp.concatenate(acc[c * per : (c + 1) * per], axis=1)

    rows.first()
    cols.first()
    sibling(0)
    row_ready(0)

    def before(k):
        if k == 0:
            rows.second()
            for s in (1, 2, 3):
                sibling(s)
            cols.second()
            for s in (1, 2, 3):
                row_ready(s)
        if k == 1:
            rows.third()
            sibling(4)
            cols.third()
            rows.fourth()
            sibling(5)
            cols.fourth()
            feat.first()
            for s in (4, 5):
                row_ready(s)
        if k == 3:
            rows.last()
            for s in (6, 7):
                sibling(s)
            cols.last()
            for s in (6, 7):
                row_ready(s)
        if k == 4:
            feat.second()

    def rect(k, carry):
        first, count_r, lead, count_c = (pick(k, [r[f] for r in RECTS]) for f in range(4))
        for j in (0, 1, 3, 4):
            @pl.when(k == j)
            def _():
                before(j)

        def inner_c(cc, carry2):
            def inner_r(rr, carry3):
                pair(first + rr, lead + cc)
                return carry3

            return lax.fori_loop(0, count_r, inner_r, carry2)

        return lax.fori_loop(0, count_c, inner_c, carry)

    lax.fori_loop(0, len(RECTS), rect, 0)

    for q in range(8):
        cm[q : q + 1, :] = jnp.sum(cs[q], axis=0, keepdims=True)
    for s in range(1, 8):
        dx, e = PLACES[s]
        send(lambda s=s, dx=dx, e=e: (cm, tr.at[s], tr_s.at[s], tr_r.at[s], cpeer(dx, e)))
    feat.third()
    feat.fourth()
    for s in range(1, 8):
        arrived(tr.at[s], tr_r.at[s])

    def factor(q):
        total = cm[q : q + 1, :]
        for s in range(1, 8):
            p = SLOT[((PLACES[q][0] + PLACES[s][0]) % 2, (PLACES[q][1] - PLACES[s][1]) % 4)]
            total = total + tr[s, p : p + 1, :]
        return 0.5 / total

    al[...] = jnp.broadcast_to(factor(0), al.shape)
    ral[0, 0] = al[...]
    for i in ORDER:
        dx, e = PLACES[i]
        for h in (1, 0):
            if i + h > 0:
                send(lambda i=i, h=h, dx=dx, e=e: (al, ral.at[i, h], al_s.at[i, h], ral_r.at[i, h], rpeer(dx, e, h)))
    for q in range(8):
        cv[0:1, q * own : (q + 1) * own] = ca[q, 1:2, :]
        cv[1:2, q * own : (q + 1) * own] = al[0:1, :] if q == 0 else factor(q)
    feat.last()
    step_r, step_c = 64, 256

    def weigh(i, w_ref):
        for r in range(2 * own // step_r):
            if r * step_r % own == 0:
                ar = jnp.transpose(ral[i, r * step_r // own])[:, 0:1]
            lo = r * step_r % own
            a_r = jnp.broadcast_to(ar[lo : lo + step_r], (step_r, 128))
            a_r = jnp.concatenate([a_r] * (step_c // 128), axis=1)
            at = slice(r * step_r, (r + 1) * step_r)
            c_r = jnp.concatenate([rc[i, at, :]] * (step_c // 128), axis=1)
            for c in range(every // step_c):
                sl = slice(c * step_c, (c + 1) * step_c)
                d = t_ref[i, at, sl]
                v = jnp.exp2(d * c_r) * a_r + jnp.exp2(d * cv[0:1, sl]) * cv[1:2, sl]
                w_ref[at, sl] = v.astype(BF16)

    def order(j):
        return pick(j, ORDER)

    def to_sibling(i):
        return remote(
            t_ref.at[i, pl.ds(own, own), pl.ds(0, feats)], sr.at[i], sr_s.at[i], sr_r.at[i], rpeer(0, 0, 1)
        )

    def to_owner(i):
        dx, e = pick(i, [p[0] for p in PLACES]), pick(i, [p[1] for p in PLACES])
        b = pick(i, BACK)
        return remote(ob.at[i], obr.at[b], ob_s.at[i], ob_r.at[b], rpeer(dx, 4 - e, 0))

    def give_sibling(i, part):
        t_ref[i, own : 2 * own, 0:feats] = part
        to_sibling(i).start()

    def finish(j):
        i = order(j)
        arrived(sr.at[i], sr_r.at[i])
        ob[i] = (sr[i] + mn[j % 2]).astype(BF16)
        to_owner(i).start()

    def await_factors(i):
        for h in range(2):
            @pl.when(i + h > 0)
            def _():
                arrived(ral.at[i, h], ral_r.at[i, h])

    def multiply(w_ref):
        return jnp.dot(w_ref[...], fb[...].reshape(every, feats), preferred_element_type=F32)

    def hand_out(j, part):
        i = order(j)
        give_sibling(i, part[own:])
        mn[j % 2] = part[:own]

        @pl.when(j == 0)
        def _():
            t_ref[0, 0:own, 0:feats] = part[:own]

        @pl.when(j > 1)
        def _():
            finish(j - 1)

    def out_step(j, carry):
        i = order(j)
        await_factors(i)
        weigh(i, w0)
        hand_out(j, multiply(w0))
        return carry

    lax.fori_loop(0, 8, out_step, 0)
    finish(row * 0 + 7)
    result = t_ref[0, 0:own, 0:feats]
    arrived(sr.at[0], sr_r.at[0])
    result = result + sr[0]
    for i in ORDER[1:]:
        arrived(obr.at[i], ob_r.at[i])
        result = result + obr[i].astype(F32)
    out_ref[...] = result
    for make in started:
        remote(*make()).wait_send()

    def drain(i, carry):
        to_sibling(i).wait_send()

        @pl.when(i > 0)
        def _():
            to_owner(i).wait_send()
        return carry

    lax.fori_loop(0, 8, drain, 0)


def shards(embeddings, spread, features, block_list, list_pairs):
    own, wide = embeddings.shape
    feats = features.shape[1]
    anywhere = pl.BlockSpec(memory_space=pl.ANY)
    scalars = pl.BlockSpec(memory_space=pltpu.SMEM)
    whole = pl.BlockSpec(memory_space=pltpu.VMEM)
    vmem, dma = pltpu.VMEM, pltpu.SemaphoreType.DMA
    return pl.pallas_call(
        kernel,
        out_shape=jax.ShapeDtypeStruct((own, feats), F32),
        in_specs=[anywhere] * 2 + [whole] + [scalars] * 2,
        out_specs=whole,
        scratch_shapes=[
            vmem((8, 2, own, wide), BF16),
            vmem((8, own, wide), BF16),
            vmem((8, own, feats), BF16),
            vmem((8, 2 * own, 8 * own), F32),
            vmem((8, 2 * own, 128), F32),
            vmem((8, 2 * own, 128), F32),
            vmem((8, 2, 8, own), F32),
            vmem((8, 8, own), F32),
            vmem((8, 8, own), F32),
            vmem((8, 8, own), F32),
            vmem((8, own), F32),
            vmem((8, 2, 8, own), F32),
            vmem((8, own), F32),
            vmem((8, 8 * own), F32),
            vmem((2 * own, 8 * own), BF16),
            vmem((2, own, feats), F32),
            vmem((8, own, feats), F32),
            vmem((8, own, feats), BF16),
            vmem((8, own, feats), BF16),
            pltpu.SMEM((32,), jnp.int32),
            pltpu.SMEM((16,), jnp.int32),
            dma((3,)),
            dma((9, 2)), dma((8, 3)), dma((8, 2)), dma((8, 2)),
            dma((9, 2)), dma((8, 3)), dma((9, 2)), dma((8, 3)),
            dma((8,)), dma((8,)),
            dma((8, 2)), dma((8, 2)),
            dma((8,)), dma((8,)), dma((8,)), dma((8,)),
        ],
        compiler_params=pltpu.CompilerParams(
            collective_id=0, has_side_effects=True, vmem_limit_bytes=61 * 2**20
        ),
        name="affinities",
    )(embeddings, features, spread, block_list, list_pairs)


def solution(mesh):
    return jax.shard_map(
        shards,
        mesh=mesh,
        in_specs=(P(("row", "col"), None), P(("row", "col")), P(("row", "col"), None), P(), P()),
        out_specs=P(("row", "col"), None),
        check_vma=False,
    )
```

```python
import math

import jax
import jax.numpy as jnp
from jax import lax
from jax.experimental import pallas as pl
from jax.experimental.pallas import tpu as pltpu
from jax.sharding import PartitionSpec as P

BLK = 128
F32 = jnp.float32
BF16 = jnp.bfloat16
LOG2E = math.log2(math.e)
INF = float("inf")
MESH = pl.DeviceIdType.MESH

PLACES = ((0, 0), (1, 0), (0, 1), (0, 3), (0, 2), (1, 1), (1, 3), (1, 2))
SLOT = {p: s for s, p in enumerate(PLACES)}
ORDER = (0, 4, 7, 6, 5, 1, 2, 3)
BACK = [SLOT[(dx, (4 - e) % 4)] for dx, e in PLACES]
RECTS = ((0, 2, 0, 2), (2, 1, 0, 2), (0, 3, 2, 1), (0, 3, 3, 1), (3, 1, 0, 4))


def pick(i, values):
    return sum((i == s).astype(jnp.int32) * v for s, v in enumerate(values) if v)


def kernel(
    x_ref, f_ref, rate_ref, bl_ref, lp_ref, out_ref,
    rx, cx, fb, t_ref, rn, rc, ra, ca, cs, tr, al, ral, cm, cv, w0, mn, sr, ob, obr, rl, cl,
    loc, rx_s, rx_r, dd_s, dd_r, cx_s, cx_r, fb_s, fb_r, tr_s, tr_r,
    al_s, ral_r, sr_s, sr_r, ob_s, ob_r,
):
    own, wide = x_ref.shape
    feats = f_ref.shape[1]
    every = 8 * own
    row = lax.axis_index("row")
    col = lax.axis_index("col")
    xl, y, core = col // 8, (col // 2) % 4, col % 2
    z, xh = row // 2, row % 2

    def rpeer(dx, dy, dk):
        return {"col": ((xl + dx) % 2) * 8 + ((y + dy + 4) % 4) * 2 + (core + dk) % 2}

    def cpeer(dx, dz):
        return {
            "row": ((z + dz + 4) % 4) * 2 + (xh + dx) % 2,
            "col": ((xl + dx) % 2) * 8 + y * 2 + core,
        }

    barrier = pltpu.get_barrier_semaphore()
    met = [rpeer(0, 0, 1), rpeer(1, 0, 0), rpeer(0, 1, 0), rpeer(0, -1, 0)]
    met += [cpeer(1, 0), cpeer(0, 1), cpeer(0, -1)]
    for to in met:
        pl.semaphore_signal(barrier, inc=1, device_id=to, device_id_type=MESH)

    locals_ = [
        pltpu.make_async_copy(x_ref, rx.at[0, 0], loc.at[0]),
        pltpu.make_async_copy(x_ref, cx.at[0], loc.at[1]),
        pltpu.make_async_copy(f_ref, fb.at[0], loc.at[2]),
    ]
    for c in locals_:
        c.start()

    for i, (dx, e) in enumerate(PLACES):
        for h in range(2):
            owner = row * 16 + rpeer(dx, -e, h)["col"]
            for b in range(2):
                rl[i * 4 + h * 2 + b] = bl_ref[owner * 2 + b]
        owner = cpeer(dx, -e)["row"] * 16 + cpeer(dx, -e)["col"]
        for b in range(2):
            cl[i * 2 + b] = bl_ref[owner * 2 + b]
    cs[...] = jnp.zeros_like(cs)

    locals_[0].wait()
    xf = rx[0, 0].astype(F32)
    norm = jnp.sum(xf * xf, axis=1, keepdims=True) * 0.5
    norm = jnp.transpose(jnp.broadcast_to(norm, (own, 128)))
    ra[0, 0, 0:1, :] = norm[0:1, :]
    rate = rate_ref[...].astype(F32).reshape(1, own) * (-2.0 * LOG2E)
    ra[0, 0, 1:8, :] = jnp.broadcast_to(rate, (7, own))
    ca[0] = ra[0, 0]
    for c in locals_[1:]:
        c.wait()

    pl.semaphore_wait(barrier, len(met))

    started = []

    def remote(src, dst, ssem, rsem, to):
        return pltpu.make_async_remote_copy(
            src_ref=src, dst_ref=dst, send_sem=ssem, recv_sem=rsem, device_id=to, device_id_type=MESH
        )

    def send(make):
        remote(*make()).start()
        started.append(make)

    def arrived(dst, rsem):
        remote(dst, dst, rsem, rsem, rpeer(0, 0, 1)).wait_recv()

    class Gather:
        def __init__(self, view, side, ssem, rsem, peer, size):
            self.view, self.side, self.peer, self.size = view, side, peer, size
            self.ssem, self.rsem = ssem, rsem

        def move(self, m, a, b, part, to):
            n = self.size if part is None else self.size // 2
            lo = self.size // 2 if part == 1 else 0
            send(lambda: (self.view(a, lo, n), self.view(b, lo, n), self.ssem.at[m, 0], self.rsem.at[b, part or 0], self.peer(*to)))
            if self.side is not None and part != 1:
                send(lambda: (self.side(a), self.side(b), self.ssem.at[m, 1], self.rsem.at[b, 2], self.peer(*to)))

        def first(self):
            self.move(1, 0, SLOT[(0, 1)], None, (0, 1))
            self.move(2, 0, SLOT[(0, 3)], None, (0, -1))
            self.move(0, 0, SLOT[(1, 0)], None, (1, 0))

        def second(self):
            self.recv(SLOT[(0, 1)])
            self.recv(SLOT[(0, 3)])
            self.move(3, SLOT[(0, 1)], SLOT[(0, 2)], 0, (0, 1))
            self.move(4, SLOT[(0, 3)], SLOT[(0, 2)], 1, (0, -1))
            self.move(6, SLOT[(0, 1)], SLOT[(1, 1)], None, (1, 0))
            self.recv(SLOT[(1, 0)])
            self.move(5, SLOT[(1, 0)], SLOT[(1, 3)], None, (0, -1))

        def third(self):
            self.recv(SLOT[(0, 2)])
            self.move(7, SLOT[(0, 2)], SLOT[(1, 2)], 0, (1, 0))

        def fourth(self):
            self.recv(SLOT[(1, 1)])
            self.move(8, SLOT[(1, 1)], SLOT[(1, 2)], 1, (0, 1))

        def last(self):
            self.recv(SLOT[(1, 3)])
            self.recv(SLOT[(1, 2)])

        def recv(self, slot):
            if PLACES[slot][1] == 2:
                n = self.size // 2
                arrived(self.view(slot, 0, n), self.rsem.at[slot, 0])
                arrived(self.view(slot, n, n), self.rsem.at[slot, 1])
            else:
                arrived(self.view(slot, 0, self.size), self.rsem.at[slot, 0])
            if self.side is not None:
                arrived(self.side(slot), self.rsem.at[slot, 2])

    rows = Gather(lambda s, lo, n: rx.at[s, 0, pl.ds(lo, n)], lambda s: ra.at[s, 0], rx_s, rx_r, lambda dx, d: rpeer(dx, d, 0), own)
    cols = Gather(lambda s, lo, n: cx.at[s, pl.ds(lo, n)], lambda s: ca.at[s], cx_s, cx_r, cpeer, own)
    feat = Gather(lambda s, lo, n: fb.at[s, pl.ds(lo, n)], None, fb_s, fb_r, cpeer, own)

    def sibling(slot):
        send(lambda: (rx.at[slot, 0], rx.at[slot, 1], dd_s.at[slot, 0], dd_r.at[slot, 0], rpeer(0, 0, 1)))
        send(lambda: (ra.at[slot, 0], ra.at[slot, 1], dd_s.at[slot, 1], dd_r.at[slot, 1], rpeer(0, 0, 1)))

    def lanes(a8, k):
        return jnp.broadcast_to(jnp.transpose(a8)[:, k : k + 1], (own, 128))

    def row_terms(i, h):
        rn[i, h * own : (h + 1) * own, :] = lanes(ra[i, h], 0)
        rc[i, h * own : (h + 1) * own, :] = lanes(ra[i, h], 1)

    def row_ready(i):
        row_terms(i, 0)
        arrived(rx.at[i, 1], dd_r.at[i, 0])
        arrived(ra.at[i, 1], dd_r.at[i, 1])
        row_terms(i, 1)

    def pair(ri, qi):
        m, n = 4 * own, 2 * own
        lhs = rx[pl.ds(2 * ri, 2)].reshape(m, wide)
        rhs = cx[pl.ds(2 * qi, 2)].reshape(n, wide)
        s = lax.dot_general(lhs, rhs, (((1,), (1,)), ((), ())), preferred_element_type=F32)
        self_pen = jnp.where(ri + qi == 0, INF, 0.0).astype(F32)
        acc = [jnp.zeros((8, BLK), F32) for _ in range(n // BLK)]
        per = own // BLK
        for b in range(m // BLK):
            base = []
            for cb in range(n // BLK):
                on = lp_ref[rl[ri * (m // BLK) + b], cl[qi * (n // BLK) + cb]]
                pen = jnp.where(on > 0, 0.0, INF).astype(F32)
                base.append(ca[2 * qi + cb // per, 0:1, (cb % per) * BLK : (cb % per + 1) * BLK] + pen)
            for r8 in range(BLK // 8):
                lo = b * BLK + r8 * 8
                at = (2 * ri + lo // (2 * own), slice(lo % (2 * own), lo % (2 * own) + 8))
                r_n = rn[at[0], at[1], :]
                for cb in range(n // BLK):
                    d = (r_n + base[cb]) - s[lo : lo + 8, cb * BLK : (cb + 1) * BLK]
                    if b == cb and b < per:
                        at_r = r8 * 8 + lax.broadcasted_iota(jnp.int32, (8, BLK), 0)
                        at_c = lax.broadcasted_iota(jnp.int32, (8, BLK), 1)
                        d = d + jnp.where(at_r == at_c, self_pen, 0.0)
                    t_ref[at[0], at[1], pl.ds(pl.multiple_of(qi * n + cb * BLK, BLK), BLK)] = d
                    rate = ca[2 * qi + cb // per, 1:2, (cb % per) * BLK : (cb % per + 1) * BLK]
                    acc[cb] = acc[cb] + jnp.exp2(d * rate)
        for c in range(2):
            cs[2 * qi + c] = cs[2 * qi + c] + jnp.concatenate(acc[c * per : (c + 1) * per], axis=1)

    rows.first()
    cols.first()
    sibling(0)
    row_ready(0)

    def before(k):
        if k == 0:
            rows.second()
            for s in (1, 2, 3):
                sibling(s)
            cols.second()
            for s in (1, 2, 3):
                row_ready(s)
        if k == 1:
            rows.third()
            sibling(4)
            cols.third()
            rows.fourth()
            sibling(5)
            cols.fourth()
            feat.first()
            for s in (4, 5):
                row_ready(s)
        if k == 3:
            rows.last()
            for s in (6, 7):
                sibling(s)
            cols.last()
        if k == 4:
            for s in (6, 7):
                row_ready(s)
            feat.second()

    def rect(k, carry):
        first, count_r, lead, count_c = (pick(k, [r[f] for r in RECTS]) for f in range(4))
        for j in (0, 1, 3, 4):
            @pl.when(k == j)
            def _():
                before(j)

        def inner_c(cc, carry2):
            def inner_r(rr, carry3):
                pair(first + rr, lead + cc)
                return carry3

            return lax.fori_loop(0, count_r, inner_r, carry2)

        return lax.fori_loop(0, count_c, inner_c, carry)

    lax.fori_loop(0, len(RECTS), rect, 0)

    for q in range(8):
        cm[q : q + 1, :] = jnp.sum(cs[q], axis=0, keepdims=True)
    for s in range(1, 8):
        dx, e = PLACES[s]
        send(lambda s=s, dx=dx, e=e: (cm, tr.at[s], tr_s.at[s], tr_r.at[s], cpeer(dx, e)))
    feat.third()
    feat.fourth()
    for s in range(1, 8):
        arrived(tr.at[s], tr_r.at[s])

    def factor(q):
        total = cm[q : q + 1, :]
        for s in range(1, 8):
            p = SLOT[((PLACES[q][0] + PLACES[s][0]) % 2, (PLACES[q][1] - PLACES[s][1]) % 4)]
            total = total + tr[s, p : p + 1, :]
        return 0.5 / total

    al[...] = jnp.broadcast_to(factor(0), al.shape)
    ral[0, 0] = al[...]
    for i in ORDER:
        dx, e = PLACES[i]
        for h in (1, 0):
            if i + h > 0:
                send(lambda i=i, h=h, dx=dx, e=e: (al, ral.at[i, h], al_s.at[i, h], ral_r.at[i, h], rpeer(dx, e, h)))
    for q in range(8):
        cv[0:1, q * own : (q + 1) * own] = ca[q, 1:2, :]
        cv[1:2, q * own : (q + 1) * own] = al[0:1, :] if q == 0 else factor(q)
    feat.last()
    step_r, step_c = 64, 256

    def weigh(i, w_ref):
        for r in range(2 * own // step_r):
            if r * step_r % own == 0:
                ar = jnp.transpose(ral[i, r * step_r // own])[:, 0:1]
            lo = r * step_r % own
            a_r = jnp.broadcast_to(ar[lo : lo + step_r], (step_r, 128))
            a_r = jnp.concatenate([a_r] * (step_c // 128), axis=1)
            at = slice(r * step_r, (r + 1) * step_r)
            c_r = jnp.concatenate([rc[i, at, :]] * (step_c // 128), axis=1)
            for c in range(every // step_c):
                sl = slice(c * step_c, (c + 1) * step_c)
                d = t_ref[i, at, sl]
                v = jnp.exp2(d * c_r) * a_r + jnp.exp2(d * cv[0:1, sl]) * cv[1:2, sl]
                w_ref[at, sl] = v.astype(BF16)

    def order(j):
        return pick(j, ORDER)

    def to_sibling(i):
        return remote(
            t_ref.at[i, pl.ds(own, own), pl.ds(0, feats)], sr.at[i], sr_s.at[i], sr_r.at[i], rpeer(0, 0, 1)
        )

    def to_owner(i):
        dx, e = pick(i, [p[0] for p in PLACES]), pick(i, [p[1] for p in PLACES])
        b = pick(i, BACK)
        return remote(ob.at[i], obr.at[b], ob_s.at[i], ob_r.at[b], rpeer(dx, 4 - e, 0))

    def give_sibling(i, part):
        t_ref[i, own : 2 * own, 0:feats] = part
        to_sibling(i).start()

    def finish(j):
        i = order(j)
        arrived(sr.at[i], sr_r.at[i])
        ob[i] = (sr[i] + mn[j % 2]).astype(BF16)
        to_owner(i).start()

    def await_factors(i):
        for h in range(2):
            @pl.when(i + h > 0)
            def _():
                arrived(ral.at[i, h], ral_r.at[i, h])

    def multiply(w_ref):
        return jnp.dot(w_ref[...], fb[...].reshape(every, feats), preferred_element_type=F32)

    def hand_out(j, part):
        i = order(j)
        give_sibling(i, part[own:])
        mn[j % 2] = part[:own]

        @pl.when(j == 0)
        def _():
            t_ref[0, 0:own, 0:feats] = part[:own]

        @pl.when(j > 1)
        def _():
            finish(j - 1)

    def out_step(j, carry):
        i = order(j)
        await_factors(i)
        weigh(i, w0)
        hand_out(j, multiply(w0))
        return carry

    lax.fori_loop(0, 8, out_step, 0)
    finish(row * 0 + 7)
    result = t_ref[0, 0:own, 0:feats]
    arrived(sr.at[0], sr_r.at[0])
    result = result + sr[0]
    for i in ORDER[1:]:
        arrived(obr.at[i], ob_r.at[i])
        result = result + obr[i].astype(F32)
    out_ref[...] = result
    for make in started:
        remote(*make()).wait_send()

    def drain(i, carry):
        to_sibling(i).wait_send()

        @pl.when(i > 0)
        def _():
            to_owner(i).wait_send()
        return carry

    lax.fori_loop(0, 8, drain, 0)


def shards(embeddings, spread, features, block_list, list_pairs):
    own, wide = embeddings.shape
    feats = features.shape[1]
    anywhere = pl.BlockSpec(memory_space=pl.ANY)
    scalars = pl.BlockSpec(memory_space=pltpu.SMEM)
    whole = pl.BlockSpec(memory_space=pltpu.VMEM)
    vmem, dma = pltpu.VMEM, pltpu.SemaphoreType.DMA
    return pl.pallas_call(
        kernel,
        out_shape=jax.ShapeDtypeStruct((own, feats), F32),
        in_specs=[anywhere] * 2 + [whole] + [scalars] * 2,
        out_specs=whole,
        scratch_shapes=[
            vmem((8, 2, own, wide), BF16),
            vmem((8, own, wide), BF16),
            vmem((8, own, feats), BF16),
            vmem((8, 2 * own, 8 * own), F32),
            vmem((8, 2 * own, 128), F32),
            vmem((8, 2 * own, 128), F32),
            vmem((8, 2, 8, own), F32),
            vmem((8, 8, own), F32),
            vmem((8, 8, own), F32),
            vmem((8, 8, own), F32),
            vmem((8, own), F32),
            vmem((8, 2, 8, own), F32),
            vmem((8, own), F32),
            vmem((8, 8 * own), F32),
            vmem((2 * own, 8 * own), BF16),
            vmem((2, own, feats), F32),
            vmem((8, own, feats), F32),
            vmem((8, own, feats), BF16),
            vmem((8, own, feats), BF16),
            pltpu.SMEM((32,), jnp.int32),
            pltpu.SMEM((16,), jnp.int32),
            dma((3,)),
            dma((9, 2)), dma((8, 3)), dma((8, 2)), dma((8, 2)),
            dma((9, 2)), dma((8, 3)), dma((9, 2)), dma((8, 3)),
            dma((8,)), dma((8,)),
            dma((8, 2)), dma((8, 2)),
            dma((8,)), dma((8,)), dma((8,)), dma((8,)),
        ],
        compiler_params=pltpu.CompilerParams(
            collective_id=0, has_side_effects=True, vmem_limit_bytes=61 * 2**20
        ),
        name="affinities",
    )(embeddings, features, spread, block_list, list_pairs)


def solution(mesh):
    return jax.shard_map(
        shards,
        mesh=mesh,
        in_specs=(P(("row", "col"), None), P(("row", "col")), P(("row", "col"), None), P(), P()),
        out_specs=P(("row", "col"), None),
        check_vma=False,
    )
```
